32 devices in a mesh: sys: 2 (over y), row: 2 (over x), col: 4 (over z), aux: 2 (over core).
Axes of the slice: x: 2, y: 2, z: 4, core: 2. Of those that a mesh axis runs over, the one named last changes fastest.
Arguments:
- coef_three: bfloat16 [4, 4, 512, 16384], P(('sys', 'row'), 'col', 'aux'), parts along dimension 0, may hold values from -6 to 6
- orbitals: bfloat16 [4, 4, 40, 128], P(('sys', 'row'), 'col'), parts along dimension 0, may hold values from -0.5 to 0.5
- density: bfloat16 [4, 4, 128, 128], P(('sys', 'row'), 'col'), parts along dimension 0, may hold values from -0.5 to 0.5
- pair_mask: int32 [4, 4, 8], P(('sys', 'row'), 'col'), parts along dimension 0, may hold values 0 or 1
Outputs:
- exch_self: float32 [4, 4, 128, 128], P(('sys', 'row'), 'col', 'aux'), parts along dimension 0
- exch_pair: float32 [4, 4, 8, 128, 128], P(('sys', 'row'), 'col', None, 'aux'), parts along dimension 0
- exch_full: float32 [4, 4, 128, 128], P(('sys', 'row'), 'col', 'aux'), parts along dimension 0
The draws below stay inside these ranges and needn't reach their ends.
There are 2 independent parts, one for each index of `sys`. The reference program is written for one: setup_inputs(seed, part) draws one part's arguments, and reference() takes and returns one part's arrays. A program takes and returns all parts, laid end to end along the dimension named above; each array names one. Nothing has to cross between parts.
Inputs may be any that keep to these rules, and one draw needn't show every extreme that they name: `pair_mask`: entries for neighbours outside the grid are drawn like the others and have no effect.
All inputs are finite; a program needn't handle non-finite values. No bound on the sum of `pair_mask` on one device may be relied on, other than what follows from the above.
Results may differ from the reference program's by a relative error of at most 0.0041.
Values may be sent and summed in bfloat16 or wider, within the bound.
A program may use at most 192 MiB of HBM per device.

```python
import jax
import jax.numpy as jnp
from jax import lax

NB = 128
Q = 512
OCC = 40
FROWS = 2
FCOLS = 4


def plant(array, key, smallest, top_value):
    spot = [jax.random.randint(jax.random.fold_in(key, axis), (), 0, length) for axis, length in enumerate(array.shape)]
    widest = array.shape.index(max(array.shape))
    beside = spot[:widest] + [(spot[widest] + 1) % array.shape[widest]] + spot[widest + 1:]
    return array.at[tuple(spot)].set(smallest).at[tuple(beside)].set(top_value)


def steps_of(stream_key, shape, cuts, smallest, high):
    def one(axis_at, shards_of):
        draws = jax.random.uniform(jax.random.fold_in(jax.random.fold_in(stream_key, 6), axis_at), (shards_of,), jnp.float32, smallest / len(cuts), high / len(cuts))
        return jnp.repeat(jnp.exp(draws), shape[axis_at] // shards_of).reshape((-1,) + (1,) * (len(shape) - axis_at - 1))

    loudness = one(*cuts[0])
    for cut in cuts[1:]:
        loudness = loudness * one(*cut)
    return loudness


def centred(own_key, dims, deviation, reach, shards=(), kind=jnp.bfloat16):
    array = deviation * jax.random.normal(own_key, dims, jnp.float32)
    if shards:
        array = array * steps_of(own_key, dims, shards, -0.22, 0.18)
    return jnp.clip(array, -reach, reach).astype(kind)


def setup_inputs(seed: int = 0, part: int = 0) -> dict:
    key_of = jax.random.split(jax.random.key(seed), 5)
    own_keys = jax.random.split(jax.random.fold_in(key_of[4], part), 5)
    return {
        "coef_three": centred(own_keys[0], (FROWS, FCOLS, Q, NB * NB), 1.0, 6.0, ((0, 2), (1, 4), (2, 2))),
        "orbitals": centred(own_keys[1], (FROWS, FCOLS, OCC, NB), NB ** -0.5, 0.5, ((0, 2), (1, 4))),
        "density": centred(own_keys[2], (FROWS, FCOLS, NB, NB), NB ** -0.5, 0.5, ((0, 2), (1, 4))),
        "pair_mask": plant((jax.random.randint(own_keys[3], (FROWS, FCOLS, 8), 0, 4) < 3).astype(jnp.int32), jax.random.fold_in(own_keys[3], 1), 0, 1),
    }


OFFSETS = ((-1, -1), (-1, 0), (-1, 1), (0, -1), (0, 1), (1, -1), (1, 0), (1, 1))


def contract(left, right):
    return lax.dot_general(left, right, (((0,), (0,)), ((), ())), preferred_element_type=jnp.float32)


def reference(coef_three, orbitals, density, pair_mask):
    count = FROWS * FCOLS
    flat_coef = coef_three.reshape(count, Q * NB, NB)
    flat_orb = orbitals.reshape(count, OCC, NB)
    flat_dens = density.reshape(count, NB, NB)

    def transform(pieces):
        coef, orb = pieces
        value = lax.dot_general(orb, coef, (((1,), (1,)), ((), ())), preferred_element_type=jnp.float32)
        return value.astype(jnp.bfloat16).reshape(OCC * Q, NB)

    def with_density(pieces):
        coef, dens = pieces
        dens_half = jnp.dot(coef, dens, preferred_element_type=jnp.float32).astype(jnp.bfloat16)
        left = dens_half.reshape(Q, NB, NB)
        right = coef.reshape(Q, NB, NB)
        return lax.dot_general(left, right, (((0, 2), (0, 1)), ((), ())), preferred_element_type=jnp.float32)

    half = lax.map(transform, (flat_coef, flat_orb))
    full_all = lax.map(with_density, (flat_coef, flat_dens))
    grid = half.reshape(FROWS, FCOLS, OCC * Q, NB)
    padded = jnp.pad(grid, ((1, 1), (1, 1), (0, 0), (0, 0)))
    self_scale = 1.0 / (Q * OCC)
    pair_scale = 1.0 / ((Q * OCC) ** 0.5)
    full_scale = 1.0 / ((Q * NB) ** 0.5)

    def blocks(index):
        rowpos = (index // FCOLS).astype(jnp.int32)
        colpos = (index % FCOLS).astype(jnp.int32)
        zero = jnp.zeros((), jnp.int32)
        mine = lax.dynamic_slice(padded, (rowpos + 1, colpos + 1, zero, zero), (1, 1, OCC * Q, NB))[0, 0]
        own = contract(mine, mine) * self_scale
        terms = []
        for offset in OFFSETS:
            other = lax.dynamic_slice(padded, (rowpos + 1 + offset[0], colpos + 1 + offset[1], zero, zero), (1, 1, OCC * Q, NB))[0, 0]
            terms.append(contract(mine, other))
        return own, jnp.stack(terms) * pair_scale

    own_all, pair_all = lax.map(blocks, jnp.arange(count, dtype=jnp.int32))
    exch_self = own_all.reshape(FROWS, FCOLS, NB, NB)
    maskf = pair_mask.astype(jnp.float32)
    exch_pair = pair_all.reshape(FROWS, FCOLS, 8, NB, NB) * maskf[:, :, :, None, None]
    exch_full = (full_all * full_scale).reshape(FROWS, FCOLS, NB, NB)
    return exch_self, exch_pair, exch_full
```

```python
import functools

import jax
import jax.numpy as jnp
from jax import lax
from jax.experimental import pallas as pl
from jax.experimental.pallas import tpu as pltpu
from jax.sharding import PartitionSpec as P

MESH = pl.DeviceIdType.MESH
LEFT, RIGHT, UP, DOWN, OWN = range(5)
OPPOSITE = (RIGHT, LEFT, DOWN, UP)
NAMES = (
    (OWN, LEFT), (OWN, RIGHT), (OWN, UP), (OWN, DOWN),
    (LEFT, UP), (LEFT, DOWN), (RIGHT, UP), (RIGHT, DOWN),
)
PLAN = (
    (((RIGHT, None), (UP, None), (DOWN, None)),
     ((OWN, LEFT), (OWN, DOWN), (LEFT, DOWN), (LEFT, UP))),
    (((LEFT, None), (UP, None), (DOWN, None)),
     ((OWN, RIGHT), (OWN, DOWN), (RIGHT, DOWN), (RIGHT, UP))),
    (((RIGHT, None), (LEFT, DOWN), (UP, None)),
     ((OWN, LEFT), (OWN, DOWN), (LEFT, DOWN), (RIGHT, DOWN))),
    (((RIGHT, UP), (LEFT, None), (DOWN, None)),
     ((OWN, RIGHT), (OWN, UP), (LEFT, UP), (RIGHT, UP))),
    (((RIGHT, DOWN), (LEFT, None), (UP, None)),
     ((OWN, RIGHT), (OWN, DOWN), (LEFT, DOWN), (RIGHT, DOWN))),
    (((RIGHT, None), (LEFT, UP), (DOWN, None)),
     ((OWN, LEFT), (OWN, UP), (LEFT, UP), (RIGHT, UP))),
)


def row_dot(left, right):
    return lax.dot_general(
        left, right, (((1,), (1,)), ((), ())), preferred_element_type=jnp.float32
    )


def cut(total):
    parts = len(PLAN)
    ends = [(total * i) // parts for i in range(parts + 1)]
    return list(zip(ends[:-1], ends[1:]))


def turn_block(stage, count, rows, store):
    lanes = stage.shape[2]
    for part in range(stage.shape[0]):
        for o in range(rows):
            piece = stage[part, pl.ds(o, count, stride=rows), :]
            store(o, slice(part * lanes, (part + 1) * lanes), piece.astype(jnp.bfloat16))


def half_kernel(orb_ref, coef_ref, out_ref, stage):
    occ, basis = orb_ref.shape
    block = out_ref.shape[1]
    lanes = stage.shape[2]
    orb = orb_ref[...]
    for m in range(block):
        value = row_dot(orb, coef_ref[:, m * basis:(m + 1) * basis])
        for part in range(stage.shape[0]):
            stage[part, m * occ:(m + 1) * occ, :] = value[:, part * lanes:(part + 1) * lanes]

    def store(o, columns, piece):
        out_ref[o, :, columns] = piece

    turn_block(stage, block, occ, store)


def half_transform(coef, orbitals):
    q_local, width = coef.shape
    occ, basis = orbitals.shape
    block = 16
    lanes = 128
    return pl.pallas_call(
        half_kernel,
        grid=(width // basis // block,),
        out_shape=jax.ShapeDtypeStruct((occ, width // basis, q_local), jnp.bfloat16),
        in_specs=[
            pl.BlockSpec((occ, basis), lambda i: (0, 0)),
            pl.BlockSpec((q_local, block * basis), lambda i: (0, i)),
        ],
        out_specs=pl.BlockSpec((occ, block, q_local), lambda i: (0, i, 0)),
        scratch_shapes=[pltpu.VMEM((q_local // lanes, block * occ, lanes), jnp.float32)],
        compiler_params=pltpu.CompilerParams(vmem_limit_bytes=24 << 20),
        name="half_transform",
    )(orbitals, coef)


def exchange_kernel(
    rows, cols, scales, half_hbm, coef_hbm, dens_ref, mask_ref,
    self_ref, pair_ref, full_ref,
    blocks, coef, stage, dens_half, acc, outbox, inbox, local, final, aux_local, aux_final,
    load_sem, send_sem, recv_sem, box_send, box_recv, aux_send, aux_recv,
):
    occ, basis, q_local = half_hbm.shape
    r, c, a = lax.axis_index("row"), lax.axis_index("col"), lax.axis_index("aux")
    has = (c > 0, c < cols - 1, r > 0, r < rows - 1)
    where = ({"col": c - 1}, {"col": c + 1}, {"row": r - 1}, {"row": r + 1})
    partner = {"aux": 1 - a}
    slices = cut(occ)

    load_coef = pltpu.make_async_copy(coef_hbm, coef, load_sem.at[0])
    load_half = pltpu.make_async_copy(half_hbm, blocks.at[OWN], load_sem.at[1])
    load_half.start()
    load_coef.start()

    barrier = pltpu.get_barrier_semaphore()
    pl.semaphore_signal(barrier, inc=1, device_id=partner, device_id_type=MESH)
    for side in range(4):
        @pl.when(has[side])
        def _(side=side):
            pl.semaphore_signal(barrier, inc=1, device_id=where[side], device_id_type=MESH)
    expected = 1 + sum(flag.astype(jnp.int32) for flag in has)
    pl.semaphore_wait(barrier, expected)

    def transfer(index, side):
        start, end = slices[index]
        return pltpu.make_async_remote_copy(
            src_ref=half_hbm.at[pl.ds(start, end - start)],
            dst_ref=blocks.at[OPPOSITE[side], pl.ds(start, end - start)],
            send_sem=send_sem.at[side, index],
            recv_sem=recv_sem.at[OPPOSITE[side], index],
            device_id=where[side],
            device_id_type=MESH,
        )

    def arrival(index, side):
        start, end = slices[index]
        return pltpu.make_async_remote_copy(
            src_ref=half_hbm.at[pl.ds(start, end - start)],
            dst_ref=blocks.at[side, pl.ds(start, end - start)],
            send_sem=send_sem.at[side, index],
            recv_sem=recv_sem.at[side, index],
            device_id=where[side],
            device_id_type=MESH,
        )

    def both(first, second):
        return first if second is None else jnp.logical_and(first, second)

    def flag_of(condition):
        return None if condition is None else has[condition]

    for index, (sends, _) in enumerate(PLAN):
        for side, condition in sends:
            @pl.when(both(has[side], flag_of(condition)))
            def _(index=index, side=side):
                transfer(index, side).start()

    for index in range(len(NAMES)):
        acc[index] = jnp.zeros((basis, basis), jnp.float32)
    for side in range(4):
        @pl.when(jnp.logical_not(has[side]))
        def _(side=side):
            inbox[side] = jnp.zeros(inbox.shape[1:], jnp.float32)

    def product(first, second, start, end):
        left = jnp.concatenate([blocks[first, o] for o in range(start, end)], axis=1)
        right = jnp.concatenate([blocks[second, o] for o in range(start, end)], axis=1)
        return row_dot(left, right)

    load_half.wait()
    load_coef.wait()

    dens_turned = dens_ref[...].astype(jnp.float32).T.astype(jnp.bfloat16)
    lanes = stage.shape[2]
    block = stage.shape[1] // basis

    @pl.loop(0, basis // block)
    def _(step):
        @pl.loop(0, block)
        def _(m):
            at = pl.multiple_of((step * block + m) * basis, basis)
            value = row_dot(dens_turned, coef[:, pl.ds(at, basis)])
            to = pl.multiple_of(m * basis, basis)
            for part in range(stage.shape[0]):
                stage[part, pl.ds(to, basis), :] = value[:, part * lanes:(part + 1) * lanes]

        first = pl.multiple_of(step * block, block)

        @pl.loop(0, basis // 8)
        def _(group):
            for k in range(8):
                s = group * 8 + k
                for part in range(stage.shape[0]):
                    piece = stage[part, pl.ds(s, block, stride=basis), :]
                    dens_half[s, pl.ds(first, block), part * lanes:(part + 1) * lanes] = (
                        piece.astype(jnp.bfloat16)
                    )

    local[0] = jnp.zeros((basis, basis), jnp.float32)
    local[1] = jnp.zeros((basis, basis), jnp.float32)

    @pl.loop(0, basis // 8)
    def _(group):
        left = jnp.concatenate([dens_half[group * 8 + k] for k in range(8)], axis=1)
        right = jnp.concatenate(
            [
                coef[:, pl.ds(pl.multiple_of((group * 8 + k) * basis, basis), basis)]
                for k in range(8)
            ],
            axis=0,
        )
        local[1] += jnp.dot(left, right, preferred_element_type=jnp.float32)

    @pl.loop(0, occ // 8)
    def _(group):
        mine = jnp.concatenate([blocks[OWN, group * 8 + k] for k in range(8)], axis=1)
        local[0] += row_dot(mine, mine)

    rows_out = basis // 2
    theirs = pl.ds(pl.multiple_of((1 - a) * rows_out, rows_out), rows_out)
    ours = pl.ds(pl.multiple_of(a * rows_out, rows_out), rows_out)

    def to_partner(source, target, which):
        return pltpu.make_async_remote_copy(
            src_ref=source.at[:, theirs, :],
            dst_ref=target,
            send_sem=aux_send.at[which],
            recv_sem=aux_recv.at[which],
            device_id=partner,
            device_id_type=MESH,
        )

    swap_local = to_partner(local, aux_local, 0)
    swap_local.start()

    for index, (sends, products) in enumerate(PLAN):
        start, end = slices[index]
        for side, condition in sends:
            source = OPPOSITE[side]

            @pl.when(both(has[source], flag_of(condition)))
            def _(index=index, source=source):
                arrival(index, source).wait_recv()

        for first, second in products:
            there = has[second] if first == OWN else jnp.logical_and(has[first], has[second])

            @pl.when(there)
            def _(first=first, second=second, start=start, end=end):
                acc[NAMES.index((first, second))] += product(first, second, start, end)

    def post(side):
        return pltpu.make_async_remote_copy(
            src_ref=outbox.at[side],
            dst_ref=inbox.at[OPPOSITE[side]],
            send_sem=box_send.at[side],
            recv_sem=box_recv.at[OPPOSITE[side]],
            device_id=where[side],
            device_id_type=MESH,
        )

    def collect(side):
        return pltpu.make_async_remote_copy(
            src_ref=outbox.at[side],
            dst_ref=inbox.at[side],
            send_sem=box_send.at[side],
            recv_sem=box_recv.at[side],
            device_id=where[side],
            device_id_type=MESH,
        )

    def value(first, second):
        return acc[NAMES.index((first, second))]

    outbox[LEFT, 0] = value(OWN, LEFT).T
    outbox[LEFT, 1] = value(LEFT, UP)
    outbox[LEFT, 2] = value(LEFT, DOWN)
    outbox[RIGHT, 0] = value(OWN, RIGHT).T
    outbox[RIGHT, 1] = value(RIGHT, UP)
    outbox[RIGHT, 2] = value(RIGHT, DOWN)
    outbox[UP, 0] = value(OWN, UP).T
    outbox[UP, 1] = value(LEFT, UP).T
    outbox[UP, 2] = value(RIGHT, UP).T
    outbox[DOWN, 0] = value(OWN, DOWN).T
    outbox[DOWN, 1] = value(LEFT, DOWN).T
    outbox[DOWN, 2] = value(RIGHT, DOWN).T
    for side in range(4):
        @pl.when(has[side])
        def _(side=side):
            post(side).start()
    for side in range(4):
        @pl.when(has[side])
        def _(side=side):
            collect(side).wait_recv()

    final[0] = inbox[LEFT, 1] + inbox[UP, 1]
    final[1] = value(OWN, UP) + inbox[UP, 0]
    final[2] = inbox[RIGHT, 1] + inbox[UP, 2]
    final[3] = value(OWN, LEFT) + inbox[LEFT, 0]
    final[4] = value(OWN, RIGHT) + inbox[RIGHT, 0]
    final[5] = inbox[LEFT, 2] + inbox[DOWN, 1]
    final[6] = value(OWN, DOWN) + inbox[DOWN, 0]
    final[7] = inbox[RIGHT, 2] + inbox[DOWN, 2]
    swap_final = to_partner(final, aux_final, 1)
    swap_final.start()

    self_scale, pair_scale, full_scale = scales
    swap_local.wait_recv()
    self_ref[0, 0] = (local[0, ours, :] + aux_local[0]) * self_scale
    full_ref[0, 0] = (local[1, ours, :] + aux_local[1]) * full_scale
    swap_final.wait_recv()
    for d in range(8):
        factor = mask_ref[d].astype(jnp.float32)
        pair_ref[0, 0, d] = (final[d, ours, :] + aux_final[d]) * pair_scale * factor

    swap_local.wait_send()
    swap_final.wait_send()
    for side in range(4):
        @pl.when(has[side])
        def _(side=side):
            post(side).wait_send()
    for index, (sends, _) in enumerate(PLAN):
        for side, condition in sends:
            @pl.when(both(has[side], flag_of(condition)))
            def _(index=index, side=side):
                transfer(index, side).wait_send()


def local_step(rows, cols, aux, coef_three, orbitals, density, pair_mask):
    q_local, width = coef_three.shape[2:]
    occ, basis = orbitals.shape[2:]
    coef = coef_three[0, 0]
    q_total = q_local * aux
    scales = (
        1.0 / (q_total * occ), 1.0 / (q_total * occ) ** 0.5, 1.0 / (q_total * basis) ** 0.5
    )
    half = half_transform(coef, orbitals[0, 0])
    rows_out = basis // aux
    lanes = 128
    f32 = jnp.float32
    dma = pltpu.SemaphoreType.DMA
    vmem = pl.BlockSpec(memory_space=pltpu.VMEM)
    return pl.pallas_call(
        functools.partial(exchange_kernel, rows, cols, scales),
        out_shape=(
            jax.ShapeDtypeStruct((1, 1, rows_out, basis), f32),
            jax.ShapeDtypeStruct((1, 1, 8, rows_out, basis), f32),
            jax.ShapeDtypeStruct((1, 1, rows_out, basis), f32),
        ),
        in_specs=[
            pl.BlockSpec(memory_space=pl.ANY),
            pl.BlockSpec(memory_space=pl.ANY),
            vmem,
            pl.BlockSpec(memory_space=pltpu.SMEM),
        ],
        out_specs=(vmem, vmem, vmem),
        scratch_shapes=[
            pltpu.VMEM((5, occ, basis, q_local), jnp.bfloat16),
            pltpu.VMEM((q_local, width), jnp.bfloat16),
            pltpu.VMEM((q_local // lanes, 16 * basis, lanes), f32),
            pltpu.VMEM((basis, basis, q_local), jnp.bfloat16),
            pltpu.VMEM((8, basis, basis), f32),
            pltpu.VMEM((4, 3, basis, basis), f32),
            pltpu.VMEM((4, 3, basis, basis), f32),
            pltpu.VMEM((2, basis, basis), f32),
            pltpu.VMEM((8, basis, basis), f32),
            pltpu.VMEM((2, rows_out, basis), f32),
            pltpu.VMEM((8, rows_out, basis), f32),
            dma((2,)),
            dma((4, len(PLAN))),
            dma((4, len(PLAN))),
            dma((4,)),
            dma((4,)),
            dma((2,)),
            dma((2,)),
        ],
        compiler_params=pltpu.CompilerParams(
            collective_id=0, has_side_effects=True, vmem_limit_bytes=56 << 20
        ),
        name="exchange",
    )(half, coef, density[0, 0], pair_mask[0, 0])


def solution(mesh):
    in_specs = (
        P(("sys", "row"), "col", "aux", None),
        P(("sys", "row"), "col", None, None),
        P(("sys", "row"), "col", None, None),
        P(("sys", "row"), "col", None),
    )
    out_specs = (
        P(("sys", "row"), "col", "aux", None),
        P(("sys", "row"), "col", None, "aux", None),
        P(("sys", "row"), "col", "aux", None),
    )
    body = functools.partial(local_step, mesh.shape["row"], mesh.shape["col"], mesh.shape["aux"])
    return jax.shard_map(body, mesh=mesh, in_specs=in_specs, out_specs=out_specs, check_vma=False)
```

```python
import functools

import jax
import jax.numpy as jnp
from jax import lax
from jax.experimental import pallas as pl
from jax.experimental.pallas import tpu as pltpu
from jax.sharding import PartitionSpec as P

MESH = pl.DeviceIdType.MESH
LEFT, RIGHT, UP, DOWN, OWN = range(5)
OPPOSITE = (RIGHT, LEFT, DOWN, UP)
NAMES = (
    (OWN, LEFT), (OWN, RIGHT), (OWN, UP), (OWN, DOWN),
    (LEFT, UP), (LEFT, DOWN), (RIGHT, UP), (RIGHT, DOWN),
)
PLAN = (
    (((RIGHT, None), (UP, None), (DOWN, None)),
     ((OWN, LEFT), (OWN, DOWN), (LEFT, DOWN), (LEFT, UP))),
    (((LEFT, None), (UP, None), (DOWN, None)),
     ((OWN, RIGHT), (OWN, DOWN), (RIGHT, DOWN), (RIGHT, UP))),
    (((RIGHT, None), (LEFT, DOWN), (UP, None)),
     ((OWN, LEFT), (OWN, DOWN), (LEFT, DOWN), (RIGHT, DOWN))),
    (((RIGHT, UP), (LEFT, None), (DOWN, None)),
     ((OWN, RIGHT), (OWN, UP), (LEFT, UP), (RIGHT, UP))),
    (((RIGHT, DOWN), (LEFT, None), (UP, None)),
     ((OWN, RIGHT), (OWN, DOWN), (LEFT, DOWN), (RIGHT, DOWN))),
    (((RIGHT, None), (LEFT, UP), (DOWN, None)),
     ((OWN, LEFT), (OWN, UP), (LEFT, UP), (RIGHT, UP))),
)


def row_dot(left, right):
    return lax.dot_general(
        left, right, (((1,), (1,)), ((), ())), preferred_element_type=jnp.float32
    )


def cut(total):
    parts = len(PLAN)
    ends = [(total * i) // parts for i in range(parts + 1)]
    return list(zip(ends[:-1], ends[1:]))


def exchange_kernel(
    rows, cols, coef_hbm, orb_ref, dens_ref, out_ref,
    blocks, coef, stage, dens_half, acc, outbox, inbox, local, final, aux_local, aux_final,
    load_sem, send_sem, recv_sem, box_send, box_recv, aux_send, aux_recv,
):
    occ, basis = orb_ref.shape
    q_local = coef_hbm.shape[0]
    r, c, a = lax.axis_index("row"), lax.axis_index("col"), lax.axis_index("aux")
    has = (c > 0, c < cols - 1, r > 0, r < rows - 1)
    where = ({"col": c - 1}, {"col": c + 1}, {"row": r - 1}, {"row": r + 1})
    partner = {"aux": 1 - a}
    slices = cut(occ)

    parts, _, lanes = stage.shape
    block = stage.shape[1] // basis
    steps = basis // block

    def load(part, step):
        to = pl.multiple_of(step * (block * basis), block * basis)
        piece = (pl.ds(part * lanes, lanes), pl.ds(to, block * basis))
        return pltpu.make_async_copy(
            coef_hbm.at[piece], coef.at[piece], load_sem.at[part, step]
        )

    for part in range(parts):
        for step in range(steps):
            load(part, step).start()

    barrier = pltpu.get_barrier_semaphore()
    pl.semaphore_signal(barrier, inc=1, device_id=partner, device_id_type=MESH)
    for side in range(4):
        @pl.when(has[side])
        def _(side=side):
            pl.semaphore_signal(barrier, inc=1, device_id=where[side], device_id_type=MESH)
    expected = 1 + sum(flag.astype(jnp.int32) for flag in has)
    pl.semaphore_wait(barrier, expected)

    def copy(index, part, side, slot):
        start, end = slices[index]
        piece = (pl.ds(start, end - start), slice(None), pl.ds(part * lanes, lanes))
        return pltpu.make_async_remote_copy(
            src_ref=blocks.at[(OWN,) + piece],
            dst_ref=blocks.at[(slot,) + piece],
            send_sem=send_sem.at[side, index, part],
            recv_sem=recv_sem.at[slot, index, part],
            device_id=where[side],
            device_id_type=MESH,
        )

    def transfer(index, part, side):
        return copy(index, part, side, OPPOSITE[side])

    def arrival(index, part, side):
        return copy(index, part, side, side)

    def both(first, second):
        return first if second is None else jnp.logical_and(first, second)

    def flag_of(condition):
        return None if condition is None else has[condition]

    orb = orb_ref[...]
    for part in range(parts):
        @pl.loop(0, steps)
        def _(step, part=part):
            load(part, step).wait()
            for m in range(block):
                at = pl.multiple_of((step * block + m) * basis, basis)
                stage[part, m * occ:(m + 1) * occ, :] = row_dot(
                    orb, coef[part * lanes:(part + 1) * lanes, pl.ds(at, basis)]
                )
            first = pl.multiple_of(step * block, block)
            for o in range(occ):
                piece = stage[part, pl.ds(o, block, stride=occ), :]
                blocks[OWN, o, pl.ds(first, block), part * lanes:(part + 1) * lanes] = (
                    piece.astype(jnp.bfloat16)
                )

        for index, (sends, _) in enumerate(PLAN):
            for side, condition in sends:
                @pl.when(both(has[side], flag_of(condition)))
                def _(index=index, part=part, side=side):
                    transfer(index, part, side).start()

    for index in range(len(NAMES)):
        acc[index] = jnp.zeros((basis, basis), jnp.float32)
    for side in range(4):
        @pl.when(jnp.logical_not(has[side]))
        def _(side=side):
            inbox[side] = jnp.zeros(inbox.shape[1:], jnp.float32)

    def product(first, second, start, end):
        left = jnp.concatenate([blocks[first, o] for o in range(start, end)], axis=1)
        right = jnp.concatenate([blocks[second, o] for o in range(start, end)], axis=1)
        return row_dot(left, right)

    dens_turned = dens_ref[...].astype(jnp.float32).T.astype(jnp.bfloat16)

    @pl.loop(0, steps)
    def _(step):
        for m in range(block):
            at = pl.multiple_of((step * block + m) * basis, basis)
            value = row_dot(dens_turned, coef[:, pl.ds(at, basis)])
            for part in range(stage.shape[0]):
                stage[part, m * basis:(m + 1) * basis, :] = (
                    value[:, part * lanes:(part + 1) * lanes]
                )

        first = pl.multiple_of(step * block, block)

        @pl.loop(0, basis // 8)
        def _(group):
            for k in range(8):
                s = group * 8 + k
                for part in range(stage.shape[0]):
                    piece = stage[part, pl.ds(s, block, stride=basis), :]
                    dens_half[s, pl.ds(first, block), part * lanes:(part + 1) * lanes] = (
                        piece.astype(jnp.bfloat16)
                    )

    local[0] = jnp.zeros((basis, basis), jnp.float32)
    local[1] = jnp.zeros((basis, basis), jnp.float32)

    @pl.loop(0, basis // 8)
    def _(group):
        left = jnp.concatenate([dens_half[group * 8 + k] for k in range(8)], axis=1)
        right = jnp.concatenate(
            [
                coef[:, pl.ds(pl.multiple_of((group * 8 + k) * basis, basis), basis)]
                for k in range(8)
            ],
            axis=0,
        )
        local[1] += jnp.dot(left, right, preferred_element_type=jnp.float32)

    @pl.loop(0, occ // 8)
    def _(group):
        mine = jnp.concatenate([blocks[OWN, group * 8 + k] for k in range(8)], axis=1)
        local[0] += row_dot(mine, mine)

    rows_out = basis // 2
    theirs = pl.ds(pl.multiple_of((1 - a) * rows_out, rows_out), rows_out)
    ours = pl.ds(pl.multiple_of(a * rows_out, rows_out), rows_out)

    def to_partner(source, target, which):
        return pltpu.make_async_remote_copy(
            src_ref=source.at[:, theirs, :],
            dst_ref=target,
            send_sem=aux_send.at[which],
            recv_sem=aux_recv.at[which],
            device_id=partner,
            device_id_type=MESH,
        )

    swap_local = to_partner(local, aux_local, 0)
    swap_local.start()

    for index, (sends, products) in enumerate(PLAN):
        start, end = slices[index]
        for side, condition in sends:
            source = OPPOSITE[side]

            @pl.when(both(has[source], flag_of(condition)))
            def _(index=index, source=source):
                for part in range(parts):
                    arrival(index, part, source).wait_recv()

        for first, second in products:
            there = has[second] if first == OWN else jnp.logical_and(has[first], has[second])

            @pl.when(there)
            def _(first=first, second=second, start=start, end=end):
                acc[NAMES.index((first, second))] += product(first, second, start, end)

    def post(side):
        return pltpu.make_async_remote_copy(
            src_ref=outbox.at[side],
            dst_ref=inbox.at[OPPOSITE[side]],
            send_sem=box_send.at[side],
            recv_sem=box_recv.at[OPPOSITE[side]],
            device_id=where[side],
            device_id_type=MESH,
        )

    def collect(side):
        return pltpu.make_async_remote_copy(
            src_ref=outbox.at[side],
            dst_ref=inbox.at[side],
            send_sem=box_send.at[side],
            recv_sem=box_recv.at[side],
            device_id=where[side],
            device_id_type=MESH,
        )

    def value(first, second):
        return acc[NAMES.index((first, second))]

    outbox[LEFT, 0] = value(OWN, LEFT).T
    outbox[LEFT, 1] = value(LEFT, UP)
    outbox[LEFT, 2] = value(LEFT, DOWN)
    outbox[RIGHT, 0] = value(OWN, RIGHT).T
    outbox[RIGHT, 1] = value(RIGHT, UP)
    outbox[RIGHT, 2] = value(RIGHT, DOWN)
    outbox[UP, 0] = value(OWN, UP).T
    outbox[UP, 1] = value(LEFT, UP).T
    outbox[UP, 2] = value(RIGHT, UP).T
    outbox[DOWN, 0] = value(OWN, DOWN).T
    outbox[DOWN, 1] = value(LEFT, DOWN).T
    outbox[DOWN, 2] = value(RIGHT, DOWN).T
    for side in range(4):
        @pl.when(has[side])
        def _(side=side):
            post(side).start()
    for side in range(4):
        @pl.when(has[side])
        def _(side=side):
            collect(side).wait_recv()

    final[0] = inbox[LEFT, 1] + inbox[UP, 1]
    final[1] = value(OWN, UP) + inbox[UP, 0]
    final[2] = inbox[RIGHT, 1] + inbox[UP, 2]
    final[3] = value(OWN, LEFT) + inbox[LEFT, 0]
    final[4] = value(OWN, RIGHT) + inbox[RIGHT, 0]
    final[5] = inbox[LEFT, 2] + inbox[DOWN, 1]
    final[6] = value(OWN, DOWN) + inbox[DOWN, 0]
    final[7] = inbox[RIGHT, 2] + inbox[DOWN, 2]
    swap_final = to_partner(final, aux_final, 1)
    swap_final.start()

    swap_local.wait_recv()
    out_ref[8] = local[0, ours, :] + aux_local[0]
    out_ref[9] = local[1, ours, :] + aux_local[1]
    swap_final.wait_recv()
    for d in range(8):
        out_ref[d] = final[d, ours, :] + aux_final[d]

    swap_local.wait_send()
    swap_final.wait_send()
    for side in range(4):
        @pl.when(has[side])
        def _(side=side):
            post(side).wait_send()
    for index, (sends, _) in enumerate(PLAN):
        for side, condition in sends:
            @pl.when(both(has[side], flag_of(condition)))
            def _(index=index, side=side):
                for part in range(parts):
                    transfer(index, part, side).wait_send()


def finish_kernel(scales, sums_ref, mask_ref, self_ref, pair_ref, full_ref):
    self_scale, pair_scale, full_scale = scales
    for d in range(8):
        factor = mask_ref[d].astype(jnp.float32)
        pair_ref[0, 0, d] = sums_ref[d] * pair_scale * factor
    self_ref[0, 0] = sums_ref[8] * self_scale
    full_ref[0, 0] = sums_ref[9] * full_scale


def local_step(rows, cols, aux, coef_three, orbitals, density, pair_mask):
    q_local, width = coef_three.shape[2:]
    occ, basis = orbitals.shape[2:]
    coef = coef_three[0, 0]
    q_total = q_local * aux
    scales = (
        1.0 / (q_total * occ), 1.0 / (q_total * occ) ** 0.5, 1.0 / (q_total * basis) ** 0.5
    )
    rows_out = basis // aux
    lanes = 128
    f32 = jnp.float32
    dma = pltpu.SemaphoreType.DMA
    vmem = pl.BlockSpec(memory_space=pltpu.VMEM)
    sums = pl.pallas_call(
        functools.partial(exchange_kernel, rows, cols),
        out_shape=jax.ShapeDtypeStruct((10, rows_out, basis), f32),
        in_specs=[
            pl.BlockSpec(memory_space=pl.ANY),
            vmem,
            vmem,
        ],
        out_specs=vmem,
        scratch_shapes=[
            pltpu.VMEM((5, occ, basis, q_local), jnp.bfloat16),
            pltpu.VMEM((q_local, width), jnp.bfloat16),
            pltpu.VMEM((q_local // lanes, 16 * basis, lanes), f32),
            pltpu.VMEM((basis, basis, q_local), jnp.bfloat16),
            pltpu.VMEM((8, basis, basis), f32),
            pltpu.VMEM((4, 3, basis, basis), f32),
            pltpu.VMEM((4, 3, basis, basis), f32),
            pltpu.VMEM((2, basis, basis), f32),
            pltpu.VMEM((8, basis, basis), f32),
            pltpu.VMEM((2, rows_out, basis), f32),
            pltpu.VMEM((8, rows_out, basis), f32),
            dma((q_local // lanes, basis // 16)),
            dma((4, len(PLAN), q_local // lanes)),
            dma((4, len(PLAN), q_local // lanes)),
            dma((4,)),
            dma((4,)),
            dma((2,)),
            dma((2,)),
        ],
        compiler_params=pltpu.CompilerParams(
            collective_id=0, has_side_effects=True, vmem_limit_bytes=56 << 20
        ),
        name="exchange",
    )(coef, orbitals[0, 0], density[0, 0])
    return pl.pallas_call(
        functools.partial(finish_kernel, scales),
        out_shape=(
            jax.ShapeDtypeStruct((1, 1, rows_out, basis), f32),
            jax.ShapeDtypeStruct((1, 1, 8, rows_out, basis), f32),
            jax.ShapeDtypeStruct((1, 1, rows_out, basis), f32),
        ),
        in_specs=[vmem, pl.BlockSpec(memory_space=pltpu.SMEM)],
        out_specs=(vmem, vmem, vmem),
        name="finish",
    )(sums, pair_mask[0, 0])


def solution(mesh):
    in_specs = (
        P(("sys", "row"), "col", "aux", None),
        P(("sys", "row"), "col", None, None),
        P(("sys", "row"), "col", None, None),
        P(("sys", "row"), "col", None),
    )
    out_specs = (
        P(("sys", "row"), "col", "aux", None),
        P(("sys", "row"), "col", None, "aux", None),
        P(("sys", "row"), "col", "aux", None),
    )
    body = functools.partial(local_step, mesh.shape["row"], mesh.shape["col"], mesh.shape["aux"])
    return jax.shard_map(body, mesh=mesh, in_specs=in_specs, out_specs=out_specs, check_vma=False)
```
